32 devices in a mesh: groups: 2 (over y), row: 16 (over z, x, core).
Axes of the slice: x: 2, y: 2, z: 4, core: 2. Of those that a mesh axis runs over, the one named last changes fastest.
Arguments:
- pair_cols: bfloat16 [128, 256, 128], P(None, ('groups', 'row')), parts along dimension 1, may hold values from -410 to 410
- single: bfloat16 [256, 384], P(('groups', 'row')), parts along dimension 0, may hold values from -6 to 6
- rotation: float32 [9, 256], P(None, ('groups', 'row')), parts along dimension 1, may hold values from -1 to 1, as said below
- translation: float32 [3, 256], P(None, ('groups', 'row')), parts along dimension 1, may hold values from -6 to 6
- residue_mask: int32 [256], P('groups'), parts along dimension 0, may hold values from 0 to 1, as said below
- chain_index: int32 [256], P('groups'), parts along dimension 0, may hold values from 0 to 3, never falling along the last dimension, each value on 1 to 64 neighbouring positions
- query_weight: bfloat16 [384, 192], replicated, may hold values from -0.3125 to 0.3125
- key_weight: bfloat16 [384, 192], replicated, may hold values from -0.3125 to 0.3125
- value_weight: bfloat16 [384, 192], replicated, may hold values from -0.3125 to 0.3125
- qpoint_weight: bfloat16 [384, 144], replicated, may hold values from -0.3125 to 0.3125
- kpoint_weight: bfloat16 [384, 144], replicated, may hold values from -0.3125 to 0.3125
- vpoint_weight: bfloat16 [384, 288], replicated, may hold values from -0.3125 to 0.3125
- pair_weight: bfloat16 [12, 128], replicated, may hold values from -0.5 to 0.5
- head_weight: float32 [12], replicated, may hold values from -3 to 3
- chain_weight: float32 [12], replicated, may hold values from -6 to 6
- output_weight: bfloat16 [2112, 384], replicated, may hold values from -0.125 to 0.125
- gain_first: float32 [384], replicated, may hold values from 0.5 to 1.5
- mlp_first: bfloat16 [384, 384], replicated, may hold values from -0.3125 to 0.3125
- mlp_second: bfloat16 [384, 384], replicated, may hold values from -0.3125 to 0.3125
- mlp_third: bfloat16 [384, 384], replicated, may hold values from -0.3125 to 0.3125
- gain_second: float32 [384], replicated, may hold values from 0.5 to 1.5
- frame_weight: bfloat16 [384, 6], replicated, may hold values from -0.3125 to 0.3125
Outputs:
- single_out: float32 [256, 384], P(('groups', 'row')), parts along dimension 0
- rotation_out: float32 [9, 256], P(None, ('groups', 'row')), parts along dimension 1
- translation_out: float32 [3, 256], P(None, ('groups', 'row')), parts along dimension 1
The draws below stay inside these ranges and needn't reach their ends.
There are 2 independent parts, one for each index of `groups`. The reference program is written for one: setup_inputs(seed, part) draws one part's arguments, and reference() takes and returns one part's arrays. A program takes and returns all parts, laid end to end along the dimension named above; an argument that names none is the same for every part. Nothing has to cross between parts.
Inputs may be any that keep to these rules, and one draw needn't show every extreme that they name: `residue_mask`: 1 on a leading run of at least three quarters of 128 positions, 0 after it. Each column is a rotation matrix, row-major.
All inputs are finite; a program needn't handle non-finite values.
Results may differ from the reference program's by a relative error of at most 0.02.
Values may be sent and summed in bfloat16 or wider, within the bound.
A program may use at most 64 MiB of HBM per device.

```python
import math
import jax
import jax.numpy as jnp
import numpy as np
from jax import lax

CS = 384
CZ = 128
H = 12
CH = 16
PQ = 4
PV = 8
RES_DEV = 8
LAYERS = 2
L = 128
CAT = 2112
N_ROW = 16


def draw_pair_cols(key, part):
    noise_base = jnp.clip(jax.random.normal(key, (L, L, CZ), jnp.float32), -6.0, 6.0)
    return noise_base.astype(jnp.bfloat16)


def draw_rotation(key, part):
    vectors = 0.8 * jax.random.normal(key, (3, L), jnp.float32)
    inverse = 1.0 / jnp.sqrt(1.0 + jnp.sum(vectors * vectors, axis=0))
    real_part = inverse
    vector_x = vectors[0] * inverse
    vector_y = vectors[1] * inverse
    vector_z = vectors[2] * inverse
    return jnp.stack([real_part * real_part + vector_x * vector_x - vector_y * vector_y - vector_z * vector_z, 2.0 * (vector_x * vector_y - real_part * vector_z), 2.0 * (vector_x * vector_z + real_part * vector_y), 2.0 * (vector_x * vector_y + real_part * vector_z), real_part * real_part - vector_x * vector_x + vector_y * vector_y - vector_z * vector_z, 2.0 * (vector_y * vector_z - real_part * vector_x), 2.0 * (vector_x * vector_z - real_part * vector_y), 2.0 * (vector_y * vector_z + real_part * vector_x), real_part * real_part - vector_x * vector_x - vector_y * vector_y + vector_z * vector_z])


def draw_residue_mask(key, part):
    length = jax.random.randint(key, (), 3 * L // 4, L + 1)
    return (jnp.arange(L) < length).astype(jnp.int32)


def steps_of(stream_key, extent, pieces, least, largest):
    level, own = 1.0, jax.random.fold_in(stream_key, 6)
    for position, parts in pieces:
        draws = jnp.exp(jax.random.uniform(jax.random.fold_in(own, position), (parts,), jnp.float32, least / len(pieces), largest / len(pieces)))
        level = level * jnp.repeat(draws, extent[position] // parts).reshape([-1 if axis == position else 1 for axis in range(len(extent))])
    return level


def split_up(number_of, total, limit, lean):
    portions = [(1 << 20) // math.isqrt(rank ** lean) + 1 for rank in range(2, number_of + 1)]
    surplus, given = total - limit - (number_of - 1), [1] * (number_of - 1)
    while surplus > 0:
        movable = [i for i in range(number_of - 1) if given[i] < limit]
        mass, budget = sum([portions[i] for i in movable]), surplus
        for i in movable:
            extra = min(limit - given[i], max(1, budget * portions[i] // mass), surplus)
            given[i] = given[i] + extra
            surplus = surplus - extra
    return np.array([limit] + given)


def uneven_parts(own_key, amount, total, reach, lean):
    if amount == 2:
        one = jax.random.randint(own_key, (), max(1, total - reach), min(reach, total - 1) + 1)
        return jnp.stack([one, total - one])
    lengths = jnp.asarray(split_up(amount, total, reach, lean), jnp.int32)
    twos = (amount - 1) // 2
    giver, sink = lengths[1:1 + 2 * twos:2], lengths[2:2 + 2 * twos:2]
    room = jnp.minimum(giver - 1, reach - sink)
    moved = jax.random.randint(jax.random.fold_in(own_key, 1), (twos,), 0, 1 << 20) % (room + 1)
    lengths = lengths.at[1:1 + 2 * twos:2].set(giver - moved).at[2:2 + 2 * twos:2].set(sink + moved)
    return lengths[jax.random.permutation(jax.random.fold_in(own_key, 2), amount)]


def centred(stream_key, dims, deviation, bound, pieces=(), held_as=jnp.bfloat16):
    factor_of = steps_of(stream_key, dims, pieces, -0.22, 0.18) if pieces else 1.0
    values = jax.random.normal(stream_key, dims, jnp.float32) * deviation * factor_of
    return jnp.minimum(jnp.maximum(values, -bound), bound).astype(held_as)


def setup_inputs(seed: int = 0, part: int = 0) -> dict:
    key_of = jax.random.split(jax.random.key(seed), 23)
    part_keys = jax.random.split(jax.random.fold_in(key_of[22], part), 23)
    return {
        "pair_cols": draw_pair_cols(jax.random.fold_in(jax.random.fold_in(key_of[22], part), 71), part),
        "single": centred(part_keys[1], (L, CS), 1.0, 6.0, ((0, 16),)),
        "rotation": draw_rotation(jax.random.fold_in(jax.random.fold_in(key_of[22], part), 71), part),
        "translation": centred(part_keys[3], (3, L), 1.5, 6.0, ((1, 16),), jnp.float32),
        "residue_mask": draw_residue_mask(jax.random.fold_in(jax.random.fold_in(key_of[22], part), 71), part),
        "chain_index": jnp.searchsorted(jnp.cumsum(uneven_parts(part_keys[5], 4, L, L // 2, 2)), jnp.arange(L), side="right").astype(jnp.int32),
        "query_weight": centred(key_of[6], (CS, H * CH), CS ** -0.5, 0.3125),
        "key_weight": centred(key_of[7], (CS, H * CH), CS ** -0.5, 0.3125),
        "value_weight": centred(key_of[8], (CS, H * CH), CS ** -0.5, 0.3125),
        "qpoint_weight": centred(key_of[9], (CS, 3 * H * PQ), CS ** -0.5, 0.3125),
        "kpoint_weight": centred(key_of[10], (CS, 3 * H * PQ), CS ** -0.5, 0.3125),
        "vpoint_weight": centred(key_of[11], (CS, 3 * H * PV), CS ** -0.5, 0.3125),
        "pair_weight": centred(key_of[12], (H, CZ), CZ ** -0.5, 0.5),
        "head_weight": centred(key_of[13], (H,), 1.0, 3.0, (), jnp.float32),
        "chain_weight": centred(key_of[14], (H,), 1.5, 6.0, (), jnp.float32),
        "output_weight": centred(key_of[15], (CAT, CS), CAT ** -0.5, 0.125),
        "gain_first": jnp.clip(1.0 + 0.1 * jax.random.normal(key_of[16], (CS,), jnp.float32), 0.5, 1.5),
        "mlp_first": centred(key_of[17], (CS, CS), CS ** -0.5, 0.3125),
        "mlp_second": centred(key_of[18], (CS, CS), CS ** -0.5, 0.3125),
        "mlp_third": centred(key_of[19], (CS, CS), CS ** -0.5, 0.3125),
        "gain_second": jnp.clip(1.0 + 0.1 * jax.random.normal(key_of[20], (CS,), jnp.float32), 0.5, 1.5),
        "frame_weight": centred(key_of[21], (CS, 6), CS ** -0.5, 0.3125),
    }


EXACT_PRODUCT = lax.Precision.HIGHEST
LOGIT_WEIGHT = (1.0 / 3.0) ** 0.5

def to_global(points, rotation, translation):
    components = []
    for component in range(3):
        components.append(rotation[3 * component][:, None] * points[:, 0] + rotation[3 * component + 1][:, None] * points[:, 1] + rotation[3 * component + 2][:, None] * points[:, 2] + translation[component][:, None])
    return jnp.stack(components, axis=1)

def to_local(points, rotation, translation):
    shifted = points - jnp.transpose(translation)[:, :, None]
    components = []
    for component in range(3):
        components.append(rotation[component][:, None] * shifted[:, 0] + rotation[3 + component][:, None] * shifted[:, 1] + rotation[6 + component][:, None] * shifted[:, 2])
    return jnp.stack(components, axis=1)

def layer_norm(values, gain_vector):
    centered = values - lax.optimization_barrier(jnp.mean(values, axis=-1, keepdims=True))
    variance = lax.optimization_barrier(jnp.mean(centered * centered, axis=-1, keepdims=True))
    return centered * lax.rsqrt(variance + 1e-05) * gain_vector

def key_side(state_bf, rotation, translation, key_weight, value_weight, kpoint_weight, vpoint_weight):
    key_count = state_bf.shape[0]
    keys_bf = jnp.dot(state_bf, key_weight, preferred_element_type=jnp.float32).astype(jnp.bfloat16)
    values_bf = jnp.dot(state_bf, value_weight, preferred_element_type=jnp.float32).astype(jnp.bfloat16)
    key_pts = jnp.dot(state_bf, kpoint_weight, preferred_element_type=jnp.float32).reshape(key_count, 3, -1)
    value_pts = jnp.dot(state_bf, vpoint_weight, preferred_element_type=jnp.float32).reshape(key_count, 3, -1)
    return (keys_bf, values_bf, to_global(key_pts, rotation, translation), to_global(value_pts, rotation, translation))

def attend(state_bf, rotation, translation, pair_rows, chain_rows, keys_bf, values_bf, key_global, value_global, chain_index, residue_mask, query_weight, qpoint_weight, pair_weight, head_weight, chain_weight):
    row_count = state_bf.shape[0]
    heads = head_weight.shape[0]
    key_count = keys_bf.shape[0]
    pair_float = pair_rows.astype(jnp.float32)
    pair_bias = jnp.einsum('ijc,hc->ihj', pair_float, pair_weight.astype(jnp.float32), precision=EXACT_PRODUCT)
    queries = jnp.dot(state_bf, query_weight, preferred_element_type=jnp.float32).astype(jnp.bfloat16).reshape(row_count, heads, -1)
    head_dim = queries.shape[2]
    query_pts = to_global(jnp.dot(state_bf, qpoint_weight, preferred_element_type=jnp.float32).reshape(row_count, 3, -1), rotation, translation)
    query_pts = query_pts.reshape(row_count, 3, heads, -1)
    key_pts = key_global.reshape(key_count, 3, heads, -1)
    point_count = query_pts.shape[3]
    scores = jnp.einsum('ihd,jhd->ihj', queries.astype(jnp.float32), keys_bf.reshape(key_count, heads, head_dim).astype(jnp.float32), precision=EXACT_PRODUCT)
    cross_term = jnp.einsum('ikhp,jkhp->ihj', query_pts, key_pts, precision=EXACT_PRODUCT)
    query_square = lax.optimization_barrier(jnp.sum(query_pts * query_pts, axis=(1, 3)))
    key_square = lax.optimization_barrier(jnp.sum(key_pts * key_pts, axis=(1, 3)))
    distance = query_square[:, :, None] + jnp.transpose(key_square)[None] - 2.0 * cross_term
    weight_c = (2.0 / (9.0 * point_count)) ** 0.5
    point_scale = jax.nn.softplus(head_weight)
    same_chain = (chain_rows[:, None] == chain_index[None, :]).astype(jnp.float32)
    logits = LOGIT_WEIGHT * (scores * head_dim ** (-0.5) + pair_bias - (0.5 * weight_c * point_scale)[None, :, None] * distance)
    logits = logits + chain_weight[None, :, None] * same_chain[:, None, :] + ((residue_mask.astype(jnp.float32) - 1.0) * 100000.0)[None, None, :]
    attention = jax.nn.softmax(logits, axis=-1).astype(jnp.bfloat16)
    attn_float = attention.astype(jnp.float32)
    outputs = jnp.einsum('ihj,jhd->ihd', attn_float, values_bf.reshape(key_count, heads, head_dim).astype(jnp.float32), precision=EXACT_PRODUCT)
    value_pts = value_global.reshape(key_count, 3, heads, -1)
    point_glob = jnp.einsum('ihj,jkhp->ikhp', attn_float, value_pts, precision=EXACT_PRODUCT)
    point_local = to_local(point_glob.reshape(row_count, 3, -1), rotation, translation)
    point_norms = jnp.sqrt(lax.optimization_barrier(jnp.sum(point_local * point_local, axis=1)) + 1e-08)
    pair_out = jnp.einsum('ihj,ijc->ihc', attn_float, pair_float, precision=EXACT_PRODUCT)
    return jnp.concatenate([outputs.reshape(row_count, -1), point_local.reshape(row_count, -1), point_norms, pair_out.reshape(row_count, -1)], axis=1).astype(jnp.bfloat16)

def frame_compose(rotation, translation, frame_update):
    inverse = lax.rsqrt(1.0 + lax.optimization_barrier(jnp.sum(frame_update[:, :3] * frame_update[:, :3], axis=1)))
    real_part = inverse
    vector_x = frame_update[:, 0] * inverse
    vector_y = frame_update[:, 1] * inverse
    vector_z = frame_update[:, 2] * inverse
    turn_matrix = [[real_part * real_part + vector_x * vector_x - vector_y * vector_y - vector_z * vector_z, 2.0 * (vector_x * vector_y - real_part * vector_z), 2.0 * (vector_x * vector_z + real_part * vector_y)], [2.0 * (vector_x * vector_y + real_part * vector_z), real_part * real_part - vector_x * vector_x + vector_y * vector_y - vector_z * vector_z, 2.0 * (vector_y * vector_z - real_part * vector_x)], [2.0 * (vector_x * vector_z - real_part * vector_y), 2.0 * (vector_y * vector_z + real_part * vector_x), real_part * real_part - vector_x * vector_x - vector_y * vector_y + vector_z * vector_z]]
    new_rotation = jnp.stack([rotation[3 * outer] * turn_matrix[0][inner] + rotation[3 * outer + 1] * turn_matrix[1][inner] + rotation[3 * outer + 2] * turn_matrix[2][inner] for outer in range(3) for inner in range(3)])
    new_translation = jnp.stack([rotation[3 * outer] * frame_update[:, 3] + rotation[3 * outer + 1] * frame_update[:, 4] + rotation[3 * outer + 2] * frame_update[:, 5] + translation[outer] for outer in range(3)])
    return (new_rotation, new_translation)

def update(single_state, concat, rotation, translation, output_weight, gain_first, mlp_first, mlp_second, mlp_third, gain_second, frame_weight):
    single_state = single_state + jnp.dot(concat, output_weight, preferred_element_type=jnp.float32)
    normed = layer_norm(single_state, gain_first)
    hidden = jax.nn.relu(jnp.dot(normed.astype(jnp.bfloat16), mlp_first, preferred_element_type=jnp.float32)).astype(jnp.bfloat16)
    hidden = jax.nn.relu(jnp.dot(hidden, mlp_second, preferred_element_type=jnp.float32)).astype(jnp.bfloat16)
    single_state = layer_norm(normed + jnp.dot(hidden, mlp_third, preferred_element_type=jnp.float32), gain_second)
    state_bf = single_state.astype(jnp.bfloat16)
    frame_update = jnp.dot(state_bf, frame_weight, preferred_element_type=jnp.float32)
    new_rotation, new_translation = frame_compose(rotation, translation, frame_update)
    return (single_state, state_bf, new_rotation, new_translation)

def reference(pair_cols, single, rotation, translation, residue_mask, chain_index, query_weight, key_weight, value_weight, qpoint_weight, kpoint_weight, vpoint_weight, pair_weight, head_weight, chain_weight, output_weight, gain_first, mlp_first, mlp_second, mlp_third, gain_second, frame_weight):
    single_state = single.astype(jnp.float32)
    state_bf = single
    for layer_index in range(LAYERS):
        keys_bf, values_bf, key_global, value_global = key_side(state_bf, rotation, translation, key_weight, value_weight, kpoint_weight, vpoint_weight)

        def one_block(block_index):
            row_start = (block_index * RES_DEV).astype(jnp.int32)
            pair_rows = lax.dynamic_slice_in_dim(pair_cols, row_start, RES_DEV, 0)
            state_rows = lax.dynamic_slice_in_dim(state_bf, row_start, RES_DEV, 0)
            rotation_rows = lax.dynamic_slice_in_dim(rotation, row_start, RES_DEV, 1)
            translation_rows = lax.dynamic_slice_in_dim(translation, row_start, RES_DEV, 1)
            chain_rows = lax.dynamic_slice_in_dim(chain_index, row_start, RES_DEV, 0)
            return attend(state_rows, rotation_rows, translation_rows, pair_rows, chain_rows, keys_bf, values_bf, key_global, value_global, chain_index, residue_mask, query_weight, qpoint_weight, pair_weight, head_weight, chain_weight)
        concat = lax.map(one_block, jnp.arange(N_ROW, dtype=jnp.int32))
        concat = concat.reshape(L, concat.shape[2])
        single_state, state_bf, rotation, translation = update(single_state, concat, rotation, translation, output_weight, gain_first, mlp_first, mlp_second, mlp_third, gain_second, frame_weight)
    return (single_state, rotation, translation)
```

```python
import functools

import jax
import jax.numpy as jnp
from jax import lax
from jax.experimental import pallas as pl
from jax.experimental.pallas import tpu as pltpu
from jax.sharding import PartitionSpec as P

(
    PAIR_COLS,
    SINGLE,
    ROTATION,
    TRANSLATION,
    RESIDUE_MASK,
    CHAIN_INDEX,
    QUERY_WEIGHT,
    KEY_WEIGHT,
    VALUE_WEIGHT,
    QPOINT_WEIGHT,
    KPOINT_WEIGHT,
    VPOINT_WEIGHT,
    PAIR_WEIGHT,
    HEAD_WEIGHT,
    CHAIN_WEIGHT,
    OUTPUT_WEIGHT,
    GAIN_FIRST,
    MLP_FIRST,
    MLP_SECOND,
    MLP_THIRD,
    GAIN_SECOND,
    FRAME_WEIGHT,
) = range(22)
LAYERS = 2
LOGIT_WEIGHT = (1.0 / 3.0) ** 0.5
LANES = 128
HALF = 64
BF = jnp.bfloat16
F32 = jnp.float32
MESH = pl.DeviceIdType.MESH


def up(value, multiple):
    return -(-value // multiple) * multiple


def iota(shape, dim):
    return lax.broadcasted_iota(jnp.int32, shape, dim)


def dot(left, right):
    return jnp.dot(left, right, preferred_element_type=F32)


def dot_t(left, right):
    return lax.dot_general(left, right, (((1,), (1,)), ((), ())), preferred_element_type=F32)


def high_low(values):
    high = values.astype(BF).astype(F32)
    return high, values - high


def layer_norm(values, gain):
    centered = values - jnp.mean(values, axis=-1, keepdims=True)
    variance = jnp.mean(centered * centered, axis=-1, keepdims=True)
    return centered * lax.rsqrt(variance + 1e-05) * gain


def columns_of(frame):
    return [frame[:, c : c + 1] for c in range(12)]


def rotate(frame, parts):
    return [
        frame[3 * c] * parts[0]
        + frame[3 * c + 1] * parts[1]
        + frame[3 * c + 2] * parts[2]
        + frame[9 + c]
        for c in range(3)
    ]


def compose(frame, upd):
    inverse = lax.rsqrt(1.0 + (upd[0] * upd[0] + upd[1] * upd[1] + upd[2] * upd[2]))
    w, x, y, z = inverse, upd[0] * inverse, upd[1] * inverse, upd[2] * inverse
    turn = [
        [w * w + x * x - y * y - z * z, 2.0 * (x * y - w * z), 2.0 * (x * z + w * y)],
        [2.0 * (x * y + w * z), w * w - x * x + y * y - z * z, 2.0 * (y * z - w * x)],
        [2.0 * (x * z - w * y), 2.0 * (y * z + w * x), w * w - x * x - y * y + z * z],
    ]
    rotation = [
        frame[3 * a] * turn[0][b] + frame[3 * a + 1] * turn[1][b] + frame[3 * a + 2] * turn[2][b]
        for a in range(3)
        for b in range(3)
    ]
    translation = [
        frame[3 * a] * upd[3] + frame[3 * a + 1] * upd[4] + frame[3 * a + 2] * upd[5] + frame[9 + a]
        for a in range(3)
    ]
    return rotation + translation


def pack_frame(frame):
    high, rest = high_low(frame)
    middle, low = high_low(rest)
    return (high + pltpu.roll(middle, 16, 1) + pltpu.roll(low, 32, 1)).astype(BF)


def unpack_frame(packed):
    return packed + pltpu.roll(packed, LANES - 16, 1) + pltpu.roll(packed, LANES - 32, 1)


def kernel(n, names, *refs):
    count = len(names)
    hbm = dict(zip(names, refs[:count]))
    single_out, rotation_out, translation_out = refs[count : count + 3]
    rest = refs[count + 3 :]
    vm = dict(zip(names[1:], rest[: count - 1]))
    (arrived, pair_buf, gat, wkv, wq, pair_w, tile, stat, pair_acc) = rest[count - 1 : -6]
    load_sem, gsend, grecv, psend, precv, own_sem = rest[-6:]

    rows, channels = vm[SINGLE].shape
    heads = vm[HEAD_WEIGHT].shape[1]
    hp = pair_w.shape[0]
    keys = n * rows
    head_dim = hbm[QUERY_WEIGHT].shape[0] // heads
    qd = up(heads * head_dim, LANES)
    pw = hbm[KPOINT_WEIGHT].shape[0] // 3
    pv = hbm[VPOINT_WEIGHT].shape[0] // 3
    points, vpoints = pw // heads, pv // heads
    me = lax.axis_index("row")

    def each_peer(body):
        if n <= 16:
            for k in range(1, n):
                body(lax.rem(me + k, n))
        else:

            def step(k, carry):
                body(lax.rem(me + k, n))
                return carry

            lax.fori_loop(1, n, step, 0)

    base_v = qd + 3 * LANES
    placed = {
        QUERY_WEIGHT: (wq, 0, heads * head_dim, 1),
        KEY_WEIGHT: (wkv, 0, heads * head_dim, 1),
        VALUE_WEIGHT: (wkv, base_v, heads * head_dim, 1),
        QPOINT_WEIGHT: (wq, qd, pw, 3),
        KPOINT_WEIGHT: (wkv, qd, pw, 3),
        VPOINT_WEIGHT: (wkv, base_v + qd, pv, 3),
    }
    loads = {}
    used = 0
    for name in names[1:]:
        if name in placed:
            target, first, size, pieces = placed[name]
            pairs = [
                (hbm[name].at[pl.ds(c * size, size)], target.at[pl.ds(first + c * LANES, size)])
                for c in range(pieces)
            ]
        else:
            pairs = [(hbm[name], vm[name])]
        loads[name] = []
        for source, target in pairs:
            loads[name].append(pltpu.make_async_copy(source, target, load_sem.at[used]))
            used += 1

    def ready(*wanted):
        for name in wanted:
            for load in loads[name]:
                load.wait()

    for name in names[1:]:
        for load in loads[name]:
            load.start()

    barrier = pltpu.get_barrier_semaphore()
    each_peer(
        lambda p: pl.semaphore_signal(barrier, inc=1, device_id={"row": p}, device_id_type=MESH)
    )

    def send_state(layer, p):
        return pltpu.make_async_remote_copy(
            src_ref=gat.at[layer, me],
            dst_ref=gat.at[layer, me],
            send_sem=gsend.at[layer, p],
            recv_sem=grecv.at[layer, me],
            device_id={"row": p},
            device_id_type=MESH,
        )

    def take_state(layer, p):
        return pltpu.make_async_remote_copy(
            src_ref=gat.at[layer, p],
            dst_ref=gat.at[layer, p],
            send_sem=gsend.at[layer, p],
            recv_sem=grecv.at[layer, p],
            device_id={"row": p},
            device_id_type=MESH,
        )

    def send_pair(p, slot):
        return pltpu.make_async_remote_copy(
            src_ref=hbm[PAIR_COLS].at[pl.ds(p * rows, rows)],
            dst_ref=arrived.at[slot],
            send_sem=psend.at[p],
            recv_sem=precv.at[slot],
            device_id={"row": p},
            device_id_type=MESH,
        )

    own_pair = pltpu.make_async_copy(
        hbm[PAIR_COLS].at[pl.ds(me * rows, rows)], arrived.at[me], own_sem
    )
    own_pair.start()

    tile[...] = jnp.zeros_like(tile)
    ready(SINGLE, ROTATION, TRANSLATION, HEAD_WEIGHT, CHAIN_WEIGHT)
    tile[0:rows, 0:9] = vm[ROTATION][...]
    lane_rows = iota((rows, LANES), 1)
    frame = jnp.where(lane_rows < 9, tile[0:rows, :], 0.0)
    tile[9:12, 0:rows] = vm[TRANSLATION][...]
    tile[12:13, 0:heads] = vm[HEAD_WEIGHT][...]
    tile[13:14, 0:heads] = vm[CHAIN_WEIGHT][...]
    turned = tile[...].T
    frame = jnp.where((lane_rows >= 9) & (lane_rows < 12), turned[0:rows], frame)
    head_col = turned[0:hp, 12:13]
    chain_col = turned[0:hp, 13:14]
    state = vm[SINGLE][...].astype(F32)
    gat[0, me, :, 0:channels] = vm[SINGLE][...]
    gat[0, me, :, channels:] = pack_frame(frame)

    pl.semaphore_wait(barrier, n - 1)
    each_peer(lambda p: send_state(0, p).start())
    each_peer(lambda p: send_pair(p, me).start())

    for target, first, size, pieces in placed.values():
        for c in range(pieces):
            start = first + c * LANES + size
            gap = up(size, LANES) - size
            if gap:
                target[start : start + gap] = jnp.zeros((gap, channels), BF)
    pair_w[...] = jnp.zeros_like(pair_w)
    ready(PAIR_WEIGHT)
    pair_w[0:heads, :] = vm[PAIR_WEIGHT][...].astype(F32)

    mask_q = (
        (iota((hp, qd), 1) // head_dim == iota((hp, qd), 0)) & (iota((hp, qd), 1) < heads * head_dim)
    ).astype(F32)
    lane_p = iota((hp, LANES), 1) % HALF
    mask_p = ((lane_p // points == iota((hp, LANES), 0)) & (lane_p < pw)).astype(F32)
    mask_once = jnp.where(iota((hp, LANES), 1) < HALF, mask_p, 0.0)
    lane_v = iota((hp, LANES), 1)
    mask_v = ((lane_v // vpoints == iota((hp, LANES), 0)) & (lane_v < pv)).astype(F32)

    def expand(values, mask):
        return (values[:, None, :] * mask[None]).reshape(rows * hp, values.shape[1])

    def collapse(values, mask):
        return jnp.sum(values.reshape(rows, hp, values.shape[1]) * mask[None], axis=1)

    def per_row(column):
        return jnp.broadcast_to(column[None], (rows, hp, 1)).reshape(rows * hp, 1)

    softplus = jnp.maximum(head_col, 0.0) + jnp.log(1.0 + jnp.exp(-jnp.abs(head_col)))
    weight_c = (2.0 / (9.0 * points)) ** 0.5
    coef = per_row(-LOGIT_WEIGHT * 0.5 * weight_c * softplus)
    mask_rows = jnp.broadcast_to(mask_p[None], (rows, hp, LANES)).reshape(rows * hp, LANES).astype(BF)

    ready(CHAIN_INDEX, RESIDUE_MASK)
    chain = vm[CHAIN_INDEX][...].astype(F32)
    at_me = iota((rows, keys), 1) == me * rows + iota((rows, keys), 0)
    chain_own = jnp.sum(jnp.where(at_me, chain, 0.0), axis=1, keepdims=True)
    same = (chain == chain_own).astype(F32)
    masked = (vm[RESIDUE_MASK][...].astype(F32) - 1.0) * 100000.0

    state_bf = vm[SINGLE][...]
    for layer in range(LAYERS):
        cols = columns_of(frame)
        if layer == 0:
            ready(QUERY_WEIGHT, QPOINT_WEIGHT)
        own = dot_t(state_bf, wq[...])
        q_rows = expand(own[:, 0:qd].astype(BF).astype(F32), mask_q).astype(BF)
        lane_own = lane_rows < pw
        q_pts = rotate(cols, [own[:, qd + c * LANES : qd + (c + 1) * LANES] for c in range(3)])
        q_pts = [jnp.where(lane_own, part, 0.0) for part in q_pts]
        square = q_pts[0] * q_pts[0] + q_pts[1] * q_pts[1] + q_pts[2] * q_pts[2]
        q_square = jnp.sum(expand(square, mask_once), axis=1, keepdims=True)
        left_high, left_low = [], []
        for part in q_pts:
            high, low = high_low(-2.0 * part)
            left_high.append(expand(high + pltpu.roll(high, HALF, 1), mask_p).astype(BF))
            left_low.append(expand(low + pltpu.roll(low, HALF, 1), mask_p).astype(BF))
        left_high = jnp.concatenate(left_high + [mask_rows], axis=1)
        left_low = jnp.concatenate(left_low, axis=1)

        each_peer(lambda p: take_state(layer, p).wait_recv())
        every = gat[layer].astype(F32).reshape(keys, channels + LANES)
        if layer == 0:
            ready(KEY_WEIGHT, KPOINT_WEIGHT, VALUE_WEIGHT, VPOINT_WEIGHT)
        kv = dot_t(every[:, 0:channels].astype(BF), wkv[...])
        key_cols = columns_of(unpack_frame(every[:, channels:]))
        k_bf = kv[:, 0:qd].astype(BF)
        v_bf = kv[:, base_v : base_v + qd].astype(BF)
        k_pts = rotate(key_cols, [kv[:, qd + c * LANES : qd + (c + 1) * LANES] for c in range(3)])
        lane_key = iota((keys, LANES), 1) < pw
        k_pts = [jnp.where(lane_key, part, 0.0) for part in k_pts]
        k_square = k_pts[0] * k_pts[0] + k_pts[1] * k_pts[1] + k_pts[2] * k_pts[2]
        right = []
        for part in k_pts + [k_square]:
            high, low = high_low(part)
            right.append((high + pltpu.roll(low, HALF, 1)).astype(BF))
        start = base_v + qd
        v_pts = rotate(
            key_cols, [kv[:, start + c * LANES : start + (c + 1) * LANES] for c in range(3)]
        )
        v_high = jnp.concatenate([part.astype(BF) for part in v_pts], axis=1)
        v_low = jnp.concatenate([high_low(part)[1].astype(BF) for part in v_pts], axis=1)
        distance = (
            q_square
            + dot_t(left_high, jnp.concatenate(right, axis=1))
            + dot_t(left_low, jnp.concatenate(right[0:3], axis=1))
        )
        scores = dot_t(q_rows, k_bf)

        if layer == 0:
            own_pair.wait()
            each_peer(lambda p: send_pair(p, p).wait_recv())
            w16 = pair_w[...].astype(BF)
            for i in range(rows):
                block = arrived[:, i].astype(F32).reshape(keys, LANES).astype(BF)
                pair_buf[i] = block
                stat[i * hp : (i + 1) * hp] = (
                    LOGIT_WEIGHT * dot_t(w16, block) + chain_col * same[i : i + 1] + masked
                )
        logits = stat[...] + (LOGIT_WEIGHT * head_dim ** (-0.5)) * scores + coef * distance
        power = jnp.exp(logits - jnp.max(logits, axis=1, keepdims=True))
        attention = (power / jnp.sum(power, axis=1, keepdims=True)).astype(BF)

        for i in range(rows):
            pair_acc[i * hp : (i + 1) * hp] = dot(attention[i * hp : (i + 1) * hp], pair_buf[i])
        outputs = collapse(dot(attention, v_bf), mask_q)
        glob = dot(attention, v_high) + dot(attention, v_low)
        shifted = [
            collapse(glob[:, c * LANES : (c + 1) * LANES], mask_v) - cols[9 + c] for c in range(3)
        ]
        local = [
            cols[c] * shifted[0] + cols[3 + c] * shifted[1] + cols[6 + c] * shifted[2]
            for c in range(3)
        ]
        norm = jnp.sqrt(local[0] * local[0] + local[1] * local[1] + local[2] * local[2] + 1e-08)
        pair_out = [pair_acc[pl.ds(h, rows, stride=hp), :].astype(BF) for h in range(heads)]

        if layer == 0:
            ready(OUTPUT_WEIGHT, GAIN_FIRST, GAIN_SECOND)
            ready(MLP_FIRST, MLP_SECOND, MLP_THIRD, FRAME_WEIGHT)
        ow = vm[OUTPUT_WEIGHT]
        at = heads * head_dim
        total = dot(outputs[:, 0:at].astype(BF), ow[0:at])
        for part in local + [norm]:
            total = total + dot(part[:, 0:pv].astype(BF), ow[at : at + pv])
            at = at + pv
        total = total + dot(jnp.concatenate(pair_out, axis=1), ow[at:])
        normed = layer_norm(state + total, vm[GAIN_FIRST][...][None])
        hidden = jnp.maximum(dot(normed.astype(BF), vm[MLP_FIRST][...]), 0.0).astype(BF)
        hidden = jnp.maximum(dot(hidden, vm[MLP_SECOND][...]), 0.0).astype(BF)
        state = layer_norm(normed + dot(hidden, vm[MLP_THIRD][...]), vm[GAIN_SECOND][...][None])
        state_bf = state.astype(BF)
        fu = dot_t(state_bf, vm[FRAME_WEIGHT][...])
        new = compose(cols, [fu[:, c : c + 1] for c in range(6)])
        frame = jnp.zeros((rows, LANES), F32)
        for c in range(12):
            frame = jnp.where(lane_rows == c, new[c], frame)
        if layer + 1 < LAYERS:
            gat[layer + 1, me, :, 0:channels] = state_bf
            gat[layer + 1, me, :, channels:] = pack_frame(frame)
            each_peer(lambda p: send_state(layer + 1, p).start())

    single_out[...] = state
    rotation_out[...] = frame[:, 0:9]
    tile[0:rows, :] = frame
    turned = tile[...].T
    translation_out[...] = turned[9:12, 0:rows]
    for layer in range(LAYERS):
        each_peer(lambda p: send_state(layer, p).wait_send())
    each_peer(lambda p: send_pair(p, me).wait_send())


ORDER = (
    PAIR_COLS,
    SINGLE,
    ROTATION,
    TRANSLATION,
    HEAD_WEIGHT,
    CHAIN_WEIGHT,
    QUERY_WEIGHT,
    QPOINT_WEIGHT,
    KEY_WEIGHT,
    KPOINT_WEIGHT,
    VALUE_WEIGHT,
    VPOINT_WEIGHT,
    PAIR_WEIGHT,
    FRAME_WEIGHT,
    CHAIN_INDEX,
    RESIDUE_MASK,
    OUTPUT_WEIGHT,
    GAIN_FIRST,
    MLP_FIRST,
    MLP_SECOND,
    MLP_THIRD,
    GAIN_SECOND,
)


def hand_out(*refs):
    for source, target in zip(refs[0:3], refs[3:6]):
        target[...] = source[...]


TURNED = (
    ROTATION,
    QUERY_WEIGHT,
    KEY_WEIGHT,
    VALUE_WEIGHT,
    QPOINT_WEIGHT,
    KPOINT_WEIGHT,
    VPOINT_WEIGHT,
    FRAME_WEIGHT,
)
PLACED = (
    QUERY_WEIGHT,
    KEY_WEIGHT,
    VALUE_WEIGHT,
    QPOINT_WEIGHT,
    KPOINT_WEIGHT,
    VPOINT_WEIGHT,
)


def on_device(*args):
    n = lax.axis_size("row")
    given = dict(enumerate(args))
    given = {k: v.reshape(1, -1) if v.ndim == 1 and k not in (GAIN_FIRST, GAIN_SECOND) else v for k, v in given.items()}
    names = list(ORDER)
    for name in TURNED:
        given[name] = given[name].T
    arrays = [given[name] for name in names]
    rows, channels = given[SINGLE].shape
    heads = given[HEAD_WEIGHT].shape[1]
    hp = up(heads, 16)
    keys = n * rows
    pair_c = given[PAIR_COLS].shape[2]
    qd = up(given[QUERY_WEIGHT].shape[0], LANES)
    stubs = PLACED
    scratch = [
        pltpu.VMEM((8, LANES) if name in stubs else given[name].shape, given[name].dtype)
        for name in names[1:]
    ] + [
        pltpu.VMEM((n, rows, rows, pair_c), BF),
        pltpu.VMEM((rows, keys, pair_c), BF),
        pltpu.VMEM((LAYERS, n, rows, channels + LANES), BF),
        pltpu.VMEM((2 * qd + 6 * LANES, channels), BF),
        pltpu.VMEM((qd + 3 * LANES, channels), BF),
        pltpu.VMEM((hp, pair_c), F32),
        pltpu.VMEM((LANES, LANES), F32),
        pltpu.VMEM((rows * hp, keys), F32),
        pltpu.VMEM((rows * hp, pair_c), F32),
        pltpu.SemaphoreType.DMA((len(names) + 5,)),
        pltpu.SemaphoreType.DMA((LAYERS, n)),
        pltpu.SemaphoreType.DMA((LAYERS, n)),
        pltpu.SemaphoreType.DMA((n,)),
        pltpu.SemaphoreType.DMA((n,)),
        pltpu.SemaphoreType.DMA,
    ]
    shapes = (
        jax.ShapeDtypeStruct((rows, channels), F32),
        jax.ShapeDtypeStruct(given[ROTATION].shape, F32),
        jax.ShapeDtypeStruct(given[TRANSLATION].shape, F32),
    )
    results = pl.pallas_call(
        functools.partial(kernel, n, names),
        name="ipa",
        out_shape=shapes,
        in_specs=[pl.BlockSpec(memory_space=pl.ANY)] * len(names),
        out_specs=[pl.BlockSpec(memory_space=pltpu.VMEM)] * 3,
        scratch_shapes=scratch,
        compiler_params=pltpu.CompilerParams(
            collective_id=0, has_side_effects=True, vmem_limit_bytes=60 * 1024 * 1024
        ),
    )(*arrays)
    state, rotation, translation = pl.pallas_call(
        hand_out,
        name="out",
        out_shape=shapes,
        in_specs=[pl.BlockSpec(memory_space=pltpu.VMEM)] * 3,
        out_specs=[pl.BlockSpec(memory_space=pltpu.VMEM)] * 3,
    )(*results)
    return state, rotation.T, translation


def solution(mesh):
    split = P(None, ("groups", "row"))
    return jax.shard_map(
        on_device,
        mesh=mesh,
        in_specs=(
            P(None, ("groups", "row"), None),
            P(("groups", "row"), None),
            split,
            split,
            P("groups"),
            P("groups"),
        )
        + (P(),) * 16,
        out_specs=(P(("groups", "row"), None), split, split),
        check_vma=False,
    )
```
